32 devices in a mesh: dp: 16 (over z, x, core), tensor: 2 (over y).
Axes of the slice: x: 2, y: 2, z: 4, core: 2. Of those that a mesh axis runs over, the one named last changes fastest.
Arguments:
- stream: bfloat16 [16, 1536, 1024], P('dp')
- validity: int32 [16], P('dp'), may hold values from 0 to 1, as said below
- norm1_gain: float32 [1024], replicated, may hold values from 0.5 to 1.5
- norm1_bias: float32 [1024], replicated, may hold values from -1.75 to 1.75
- qkv_weight: bfloat16 [1024, 3, 1024], P(None, None, 'tensor'), may hold values from -0.25 to 0.25
- qkv_bias: float32 [2, 1024], P(None, 'tensor'), may hold values from -1.75 to 1.75
- proj_weight: bfloat16 [1024, 1024], P('tensor'), may hold values from -1 to 1
- proj_bias: float32 [1024], replicated, may hold values from -1.75 to 1.75
- layer_scale1: float32 [1024], replicated, may hold values from 0.25 to 1.75
- norm2_gain: float32 [1024], replicated, may hold values from 0.5 to 1.5
- norm2_bias: float32 [1024], replicated, may hold values from -1.75 to 1.75
- fc1_weight: bfloat16 [1024, 4096], P(None, 'tensor'), may hold values from -0.1875 to 0.1875
- fc1_bias: float32 [4096], P('tensor'), may hold values from -3 to 3
- fc2_weight: bfloat16 [4096, 1024], P('tensor'), may hold values from -0.09375 to 0.09375
- fc2_bias: float32 [1024], replicated, may hold values from -1.75 to 1.75
- layer_scale2: float32 [1024], replicated, may hold values from 0.25 to 1.75
- cotangent: bfloat16 [16, 1536, 1024], P('dp'), may hold values from -6 to 6
Outputs:
- block_output: bfloat16 [16, 1536, 1024], P('dp')
- stream_grad: bfloat16 [16, 1536, 1024], P('dp')
- norm1_gain_grad: float32 [1024], replicated
- norm1_bias_grad: float32 [1024], replicated
- qkv_weight_grad: float32 [1024, 3, 1024], P(None, None, 'tensor')
- qkv_bias_grad: float32 [2, 1024], P(None, 'tensor')
- proj_weight_grad: float32 [1024, 1024], P('tensor')
- proj_bias_grad: float32 [1024], replicated
- layer_scale1_grad: float32 [1024], replicated
- norm2_gain_grad: float32 [1024], replicated
- norm2_bias_grad: float32 [1024], replicated
- fc1_weight_grad: float32 [1024, 4096], P(None, 'tensor')
- fc1_bias_grad: float32 [4096], P('tensor')
- fc2_weight_grad: float32 [4096, 1024], P('tensor')
- fc2_bias_grad: float32 [1024], replicated
- layer_scale2_grad: float32 [1024], replicated
- root_means: float32 [5], replicated
The draws below stay inside these ranges and needn't reach their ends.
Inputs may be any that keep to these rules, and one draw needn't show every extreme that they name: `validity`: each slot's flag is 1 for an image and 0 for padding; at least one slot holds an image; positions 1370 and above of every slot are padding.
All inputs are finite; a program needn't handle non-finite values.
Results may differ from the reference program's by a relative error of at most 0.02.
Values may be sent and summed in bfloat16 or wider, within the bound.
No kernel may reach another device: no remote copies, remote signals or barrier semaphores. Data moves between devices by JAX's collectives and lax.ppermute only.
A program may use at most 320 MiB of HBM per device.

```python
import jax
import jax.numpy as jnp
from jax import lax

D = 1024
HEAD_DIM = 64
FF = 4096
SEQ = 1370
PAD_UNIT = 512
SLOT_LEN = 1536
SLOTS = 16
N_TENSOR = 2


def draw_stream(key, part):
    levels = jnp.arange(SLOTS, dtype=jnp.float32) / (SLOTS - 1)
    base = jax.random.normal(key, (SLOTS, SLOT_LEN, D), jnp.float32)
    rise = 3.0 ** levels
    return (base * rise[:, None, None]).astype(jnp.bfloat16)


def draw_validity(key, part):
    raw = jax.random.randint(key, (SLOTS,), 0, 4)
    chosen = jax.random.randint(jax.random.fold_in(key, 11), (), 0, SLOTS)
    flags = jnp.where(raw < 3, 1, 0).astype(jnp.int32)
    return jnp.where(jnp.arange(SLOTS) == chosen, 1, flags).astype(jnp.int32)


def steps_of(key, shape, shards, least, high):
    level = 1.0
    for axis_at, blocks in shards:
        steps = jax.random.uniform(jax.random.fold_in(jax.random.fold_in(key, 6), axis_at), (blocks,), jnp.float32, least / len(shards), high / len(shards))
        level = level * jnp.repeat(jnp.exp(steps), shape[axis_at] // blocks).reshape((-1,) + (1,) * (len(shape) - 1 - axis_at))
    return level


def normal_values(stream_key, extent, scale, bound, cuts=(), kind=jnp.bfloat16):
    values = jax.random.normal(stream_key, extent, jnp.float32) * scale
    if len(cuts) > 0:
        values = steps_of(stream_key, extent, cuts, -0.22, 0.18) * values
    return jnp.clip(values, min=-bound, max=bound).astype(kind)


def setup_inputs(seed: int = 0) -> dict:
    seeds = jax.random.split(jax.random.key(seed), 18)
    stream = draw_stream(jax.random.fold_in(seeds[17], 71), 0)
    validity = draw_validity(jax.random.fold_in(seeds[17], 71), 0)
    norm1_gain = jnp.clip(1.0 + 0.1 * jax.random.normal(seeds[2], (D,), jnp.float32), 0.5, 1.5)
    norm1_bias = normal_values(seeds[3], (D,), 0.3, 1.75, (), jnp.float32)
    qkv_weight = normal_values(seeds[4], (D, 3, D), (D // 2) ** -0.5, 0.25, ((2, 2),))
    qkv_bias = normal_values(seeds[5], (2, D), 0.3, 1.75, ((1, 2),), jnp.float32)
    proj_weight = normal_values(seeds[6], (D, D), (D // 32) ** -0.5, 1.0, ((0, 2),))
    proj_bias = normal_values(seeds[7], (D,), 0.3, 1.75, (), jnp.float32)
    layer_scale1 = jnp.clip(1.0 + 0.15 * jax.random.normal(seeds[8], (D,), jnp.float32), 0.25, 1.75)
    norm2_gain = jnp.clip(1.0 + 0.1 * jax.random.normal(seeds[9], (D,), jnp.float32), 0.5, 1.5)
    norm2_bias = normal_values(seeds[10], (D,), 0.3, 1.75, (), jnp.float32)
    fc1_weight = normal_values(seeds[11], (D, FF), D ** -0.5, 0.1875, ((1, 2),))
    fc1_bias = normal_values(seeds[12], (FF,), 0.5, 3.0, ((0, 2),), jnp.float32)
    fc2_weight = normal_values(seeds[13], (FF, D), FF ** -0.5, 0.09375, ((0, 2),))
    fc2_bias = normal_values(seeds[14], (D,), 0.3, 1.75, (), jnp.float32)
    layer_scale2 = jnp.clip(1.0 + 0.15 * jax.random.normal(seeds[15], (D,), jnp.float32), 0.25, 1.75)
    cotangent = normal_values(seeds[16], (SLOTS, SLOT_LEN, D), 1.0, 6.0, ((0, 16),))
    return dict(stream=stream, validity=validity, norm1_gain=norm1_gain, norm1_bias=norm1_bias, qkv_weight=qkv_weight, qkv_bias=qkv_bias, proj_weight=proj_weight, proj_bias=proj_bias, layer_scale1=layer_scale1, norm2_gain=norm2_gain, norm2_bias=norm2_bias, fc1_weight=fc1_weight, fc1_bias=fc1_bias, fc2_weight=fc2_weight, fc2_bias=fc2_bias, layer_scale2=layer_scale2, cotangent=cotangent)


eps = 1e-06
high = lax.Precision.HIGHEST

@jax.custom_vjp
def low(v):
    return lax.optimization_barrier(v.astype(jnp.bfloat16)).astype(jnp.float32)

@jax.custom_vjp
def low_back(v):
    return v

def low_keep(v):
    return (low(v), None)

def low_pass(kept, grad):
    return (grad,)

def back_keep(v):
    return (v, None)

def back_low(kept, grad):
    return (low(grad),)
low.defvjp(low_keep, low_pass)
low_back.defvjp(back_keep, back_low)

def normalize(values, gain, shift):
    mean = lax.optimization_barrier(jnp.mean(values, axis=-1, keepdims=True))
    centered = values - mean
    variance = lax.optimization_barrier(jnp.mean(centered * centered, axis=-1, keepdims=True))
    return centered * lax.rsqrt(variance + eps) * gain + shift

def attend(query, keyed, valued):
    length, width = query.shape
    heads = width // HEAD_DIM
    keys = keyed.reshape(length, heads, HEAD_DIM)
    values = valued.reshape(length, heads, HEAD_DIM)
    live = (jnp.arange(length, dtype=jnp.int32) < SEQ)[None, None, :]

    def one_block(index):
        block = lax.dynamic_slice_in_dim(query, index * PAD_UNIT, PAD_UNIT, 0).reshape(PAD_UNIT, heads, HEAD_DIM)
        scores = jnp.einsum('qhd,khd->hqk', block, keys, precision=high) * HEAD_DIM ** (-0.5)
        scores = low_back(scores)
        scores = jnp.where(live, scores, -1e+30)
        probs = low(jax.nn.softmax(scores, axis=-1))
        mixed = jnp.einsum('hqk,khd->qhd', probs, values, precision=high)
        return mixed.reshape(PAD_UNIT, width)
    blocks = lax.map(jax.checkpoint(one_block), jnp.arange(length // PAD_UNIT, dtype=jnp.int32))
    return blocks.reshape(length, width)

def forward(rows_in, params):
    gain1, shift1, wqkv, bqkv, wproj, bproj, scale1, gain2, shift2, wfirst, bfirst, wsecond, bsecond, scale2 = params
    first = low(normalize(rows_in, gain1, shift1))
    local = D // N_TENSOR
    hidden = FF // N_TENSOR
    attend_parts = []
    for group in range(N_TENSOR):
        cols = slice(group * local, (group + 1) * local)
        projected = low_back(jnp.einsum('ld,dcn->lcn', low_back(first), wqkv[:, :, cols], precision=high))
        query = low(projected[:, 0] + bqkv[0, cols])
        keyed = low(projected[:, 1])
        valued = low(projected[:, 2] + bqkv[1, cols])
        mixed = low(low_back(attend(query, keyed, valued)))
        attend_parts.append(low(jnp.dot(mixed, wproj[cols, :], precision=high)))
    attended = low_back(sum(attend_parts)) + bproj
    after = rows_in + scale1 * attended
    second = low(normalize(after, gain2, shift2))
    reduce_parts = []
    for group in range(N_TENSOR):
        units = slice(group * hidden, (group + 1) * hidden)
        pre = low_back(jnp.dot(low_back(second), wfirst[:, units], precision=high)) + bfirst[units]
        active = low(jax.nn.gelu(pre, approximate=False))
        reduce_parts.append(low(jnp.dot(active, wsecond[units, :], precision=high)))
    reduced = low_back(sum(reduce_parts)) + bsecond
    result = after + scale2 * reduced
    return (result, (after, scale1 * attended, scale2 * reduced))

def reference(stream, validity, norm1_gain, norm1_bias, qkv_weight, qkv_bias, proj_weight, proj_bias, layer_scale1, norm2_gain, norm2_bias, fc1_weight, fc1_bias, fc2_weight, fc2_bias, layer_scale2, cotangent):
    params = tuple((p.astype(jnp.float32) for p in (norm1_gain, norm1_bias, qkv_weight, qkv_bias, proj_weight, proj_bias, layer_scale1, norm2_gain, norm2_bias, fc1_weight, fc1_bias, fc2_weight, fc2_bias, layer_scale2)))
    live = ((validity[:, None] == 1) & (jnp.arange(SLOT_LEN, dtype=jnp.int32)[None, :] < SEQ)).astype(jnp.float32)

    def per_slot(totals, inputs):
        rows_in, grad_rows, weight = inputs
        result, pull, extras = jax.vjp(forward, rows_in, params, has_aux=True)
        grad_in, grad_params = pull(grad_rows * weight[:, None])
        totals = jax.tree.map(lambda a, b: a + b, totals, grad_params)
        after, branch_one, branch_two = extras
        squares = jnp.stack([jnp.sum(weight[:, None] * field * field) for field in (rows_in, after, result, branch_one, branch_two)])
        return (totals, (result.astype(jnp.bfloat16), grad_in.astype(jnp.bfloat16), squares))
    zeros = jax.tree.map(jnp.zeros_like, params)
    totals, (outputs, grads_in, squares) = lax.scan(per_slot, zeros, (stream.astype(jnp.float32), cotangent.astype(jnp.float32), live))
    count = jnp.sum(validity).astype(jnp.float32)
    root_means = jnp.sqrt(lax.optimization_barrier(jnp.sum(squares, axis=0)) / (count * SEQ * D))
    return (outputs, grads_in, totals[0], totals[1], totals[2], totals[3], totals[4], totals[5], totals[6], totals[7], totals[8], totals[9], totals[10], totals[11], totals[12], totals[13], root_means)
```

```python
import jax
import jax.numpy as jnp
from jax import lax
from jax.experimental import pallas as pl
from jax.experimental.pallas import tpu as pltpu
from jax.sharding import PartitionSpec as P

HEAD_DIM = 64
SEQ = 1370
PAD_UNIT = 512


eps = 1e-06


def normalize(values, gain, shift):
    mean = jnp.mean(values, axis=-1, keepdims=True)
    centered = values - mean
    variance = jnp.mean(centered * centered, axis=-1, keepdims=True)
    inverse = lax.rsqrt(variance + eps)
    normed = centered * inverse
    return (normed * gain + shift, normed, inverse)


def normalize_back(grad_out, normed, inverse, gain):
    scaled = grad_out * gain
    centered = scaled - jnp.mean(scaled, axis=-1, keepdims=True)
    return inverse * (centered - normed * jnp.mean(scaled * normed, axis=-1, keepdims=True))


NT=(((1,),(1,)),((),()))
NN=(((1,),(0,)),((),()))
def chunks_of(n,b):
    return [(i,min(b,n-i)) for i in range(0,n,b)]
def attn_fwd(q,k,v,bq=256):
    L,W=q.shape; pairs=W//128; KL=-(-SEQ//16)*16
    def kern(q_ref,k_ref,v_ref,o_ref,lse_ref,kh_ref,vt_ref):
        lane=lax.broadcasted_iota(jnp.int32,(1,128),1)
        row=lax.broadcasted_iota(jnp.int32,(KL,128),0)
        k2=k_ref[:KL,:]; v2=v_ref[:KL,:]
        for h in range(2):
            mine=(lane//64)==h
            spare=lane==(64*(1-h))
            pad=jnp.where((row>=SEQ)&spare,-1e30,0.0).astype(jnp.bfloat16)
            kh_ref[h]=jnp.where(mine,k2,pad)
        vt=v2.T
        ones=jnp.ones((16,KL),jnp.bfloat16)
        for h in range(2):
            vt_ref[h]=jnp.concatenate([vt[h*64:(h+1)*64],ones],axis=0)
        for (s0,b) in chunks_of(L,bq):
            q2=q_ref[s0:s0+b,:]
            outs=[]
            for h in range(2):
                mine=(lane//64)==h
                spare=lane==(64*(1-h))
                qh=jnp.where(mine,q2,jnp.where(spare,1.0,0.0).astype(jnp.bfloat16))
                sT=lax.dot_general(kh_ref[h],qh,NT,preferred_element_type=jnp.float32)
                m=jnp.max(sT,axis=0,keepdims=True)
                pT=jnp.exp(sT-m).astype(jnp.bfloat16)
                acc=lax.dot_general(vt_ref[h],pT,NN,preferred_element_type=jnp.float32)
                l=acc[64:65,:]
                outs.append(acc[:64]*(1.0/l))
                lse_ref[0,h:h+1,s0:s0+b]=m+jnp.log(l)
            o_ref[s0:s0+b,:]=jnp.concatenate(outs,axis=0).T.astype(jnp.bfloat16)
    spec=pl.BlockSpec((L,128),lambda p:(0,p))
    return pl.pallas_call(kern,grid=(pairs,),in_specs=[spec]*3,
        out_specs=[spec,pl.BlockSpec((1,8,L),lambda p:(p,0,0))],
        out_shape=[jax.ShapeDtypeStruct((L,W),jnp.bfloat16),jax.ShapeDtypeStruct((pairs,8,L),jnp.float32)],
        scratch_shapes=[pltpu.VMEM((2,KL,128),jnp.bfloat16),pltpu.VMEM((2,80,KL),jnp.bfloat16)],
        compiler_params=pltpu.CompilerParams(vmem_limit_bytes=56<<20),name="attend_fwd")(q,k,v)
def attn_bwd(q,k,v,o,do,lse,bq=256):
    L,W=q.shape; pairs=W//128; KL=-(-SEQ//16)*16; QL=-(-SEQ//128)*128
    def kern(q_ref,k_ref,v_ref,o_ref,do_ref,lse_ref,dq_ref,dk_ref,dv_ref,kh_ref,vh_ref,kt_ref,dk_acc,dv_acc):
        lane=lax.broadcasted_iota(jnp.int32,(1,128),1)
        row=lax.broadcasted_iota(jnp.int32,(KL,128),0)
        zero=jnp.zeros((),jnp.bfloat16)
        k2=k_ref[:KL,:]; v2=v_ref[:KL,:]
        for h in range(2):
            mine=(lane//64)==h
            spare=lane==(64*(1-h))
            pad=jnp.where((row>=SEQ)&spare,-1e30,0.0).astype(jnp.bfloat16)
            kh_ref[h]=jnp.where(mine,k2,pad)
            vh_ref[h]=jnp.where(mine,v2,zero)
        kt_ref[...]=k2.T
        for ci,(s0,b) in enumerate(chunks_of(QL,bq)):
            q2=q_ref[s0:s0+b,:]; do2=do_ref[s0:s0+b,:]
            prod=(do2.astype(jnp.float32)*o_ref[s0:s0+b,:].astype(jnp.float32)).T
            dqs=[]; dk=None; dv=None
            for h in range(2):
                mine=(lane//64)==h
                spare=lane==(64*(1-h))
                delta=jnp.sum(prod[h*64:(h+1)*64],axis=0,keepdims=True)
                qz=jnp.where(mine,q2,zero); doz=jnp.where(mine,do2,zero)
                qh=jnp.where(mine,q2,jnp.where(spare,1.0,0.0).astype(jnp.bfloat16))
                sT=lax.dot_general(kh_ref[h],qh,NT,preferred_element_type=jnp.float32)
                pT=jnp.exp(sT-lse_ref[0,h:h+1,s0:s0+b])
                dpT=lax.dot_general(vh_ref[h],do2,NT,preferred_element_type=jnp.float32)
                ds=(pT*(dpT-delta)).astype(jnp.bfloat16)
                pb=pT.astype(jnp.bfloat16)
                dvh=lax.dot_general(pb,doz,NN,preferred_element_type=jnp.float32)
                dkh=lax.dot_general(ds,qz,NN,preferred_element_type=jnp.float32)
                dv=dvh if dv is None else dv+dvh
                dk=dkh if dk is None else dk+dkh
                dqs.append(lax.dot_general(kt_ref[h*64:(h+1)*64,:],ds,NN,preferred_element_type=jnp.float32))
            if ci==0:
                dk_acc[...]=dk; dv_acc[...]=dv
            else:
                dk_acc[...]+=dk; dv_acc[...]+=dv
            dq_ref[s0:s0+b,:]=(jnp.concatenate(dqs,axis=0).T*HEAD_DIM**-0.5).astype(dq_ref.dtype)
        dk_ref[:KL,:]=dk_acc[...].astype(dk_ref.dtype); dv_ref[:KL,:]=dv_acc[...].astype(dv_ref.dtype)
        if KL<QL:
            dk_ref[KL:,:]=jnp.zeros((QL-KL,128),dk_ref.dtype); dv_ref[KL:,:]=jnp.zeros((QL-KL,128),dv_ref.dtype)
    spec=pl.BlockSpec((L,128),lambda p:(0,p))
    ospec=pl.BlockSpec((QL,128),lambda p:(0,p))
    return pl.pallas_call(kern,grid=(pairs,),in_specs=[spec]*5+[pl.BlockSpec((1,8,L),lambda p:(p,0,0))],
        out_specs=[ospec]*3,
        out_shape=[jax.ShapeDtypeStruct((QL,W),jnp.bfloat16)]*3,
        scratch_shapes=[pltpu.VMEM((2,KL,128),jnp.bfloat16),pltpu.VMEM((2,KL,128),jnp.bfloat16),pltpu.VMEM((128,KL),jnp.bfloat16),pltpu.VMEM((KL,128),jnp.float32),pltpu.VMEM((KL,128),jnp.float32)],
        compiler_params=pltpu.CompilerParams(vmem_limit_bytes=56<<20),name="attend_bwd")(q,k,v,o,do,lse)


def shards(
    stream,
    validity,
    norm1_gain,
    norm1_bias,
    qkv_weight,
    qkv_bias,
    proj_weight,
    proj_bias,
    layer_scale1,
    norm2_gain,
    norm2_bias,
    fc1_weight,
    fc1_bias,
    fc2_weight,
    fc2_bias,
    layer_scale2,
    cotangent,
):
    slots, length, width = stream.shape
    rows = slots * length
    local = qkv_weight.shape[2]
    flat = stream.reshape(rows, width).astype(jnp.float32)
    live = (
        ((validity[:, None] == 1) & (jnp.arange(length)[None, :] < SEQ))
        .astype(jnp.float32)
        .reshape(rows, 1)
    )
    first, normed1, inverse1 = normalize(flat, norm1_gain, norm1_bias)
    first_low = first.astype(jnp.bfloat16)
    projected = jnp.einsum("rd,dcn->rcn", first_low, qkv_weight, preferred_element_type=jnp.float32)
    query = ((projected[:, 0] + qkv_bias[0]) * HEAD_DIM**-0.5).astype(jnp.bfloat16)
    keyed = projected[:, 1].astype(jnp.bfloat16)
    valued = (projected[:, 2] + qkv_bias[1]).astype(jnp.bfloat16)
    mixed_rows, logsums = attn_fwd(query, keyed, valued, 512)
    attend_share = jnp.dot(mixed_rows, proj_weight, preferred_element_type=jnp.float32)
    attended = lax.psum(attend_share.astype(jnp.bfloat16), "tensor").astype(jnp.float32) + proj_bias
    after = flat + layer_scale1 * attended
    second, normed2, inverse2 = normalize(after, norm2_gain, norm2_bias)
    second_low = second.astype(jnp.bfloat16)
    hidden_pre = jnp.dot(second_low, fc1_weight, preferred_element_type=jnp.float32) + fc1_bias
    hidden_low = jax.nn.gelu(hidden_pre, approximate=False).astype(jnp.bfloat16)
    reduce_share = jnp.dot(hidden_low, fc2_weight, preferred_element_type=jnp.float32)
    reduced = lax.psum(reduce_share.astype(jnp.bfloat16), "tensor").astype(jnp.float32) + fc2_bias
    result = after + layer_scale2 * reduced
    block_output = result.astype(jnp.bfloat16).reshape(slots, length, width)
    branch_one = layer_scale1 * attended
    branch_two = layer_scale2 * reduced
    squares = jnp.stack(
        [jnp.sum(live * field * field) for field in (flat, after, result, branch_one, branch_two)]
    )
    count = jnp.sum(validity).astype(jnp.float32)
    square_sums, slot_count = lax.psum((squares, count), "dp")
    grad_rows = cotangent.reshape(rows, width).astype(jnp.float32) * live
    grad_reduced = layer_scale2 * grad_rows
    scale2_grad = jnp.sum(grad_rows * reduced, axis=0)
    second_bias_grad = jnp.sum(grad_reduced, axis=0)
    reduced_low = grad_reduced.astype(jnp.bfloat16)
    second_weight_grad = jnp.einsum(
        "rf,rd->fd", hidden_low, reduced_low, preferred_element_type=jnp.float32
    )
    grad_hidden = jnp.einsum(
        "rd,fd->rf", reduced_low, fc2_weight, preferred_element_type=jnp.float32
    )
    _, gelu_pull = jax.vjp(lambda value: jax.nn.gelu(value, approximate=False), hidden_pre)
    grad_pre = gelu_pull(grad_hidden)[0]
    first_bias_grad = jnp.sum(grad_pre, axis=0)
    pre_low = grad_pre.astype(jnp.bfloat16)
    first_weight_grad = jnp.einsum(
        "rd,rf->df", second_low, pre_low, preferred_element_type=jnp.float32
    )
    second_share = jnp.einsum("rf,df->rd", pre_low, fc1_weight, preferred_element_type=jnp.float32)
    grad_second = lax.psum(second_share.astype(jnp.bfloat16), "tensor").astype(jnp.float32)
    gain2_grad = jnp.sum(grad_second * normed2, axis=0)
    shift2_grad = jnp.sum(grad_second, axis=0)
    grad_after = grad_rows + normalize_back(grad_second, normed2, inverse2, norm2_gain)
    grad_attend = layer_scale1 * grad_after
    scale1_grad = jnp.sum(grad_after * attended, axis=0)
    merge_bias_grad = jnp.sum(grad_attend, axis=0)
    attend_low = grad_attend.astype(jnp.bfloat16)
    merge_weight_grad = jnp.einsum(
        "rn,rd->nd", mixed_rows, attend_low, preferred_element_type=jnp.float32
    )
    grad_mixed = jnp.einsum(
        "rd,nd->rn", attend_low, proj_weight, preferred_element_type=jnp.float32
    ).astype(jnp.bfloat16)
    grad_query, grad_key, grad_value = attn_bwd(
        query, keyed, valued, mixed_rows, grad_mixed, logsums, 256
    )
    some = grad_query.shape[0]
    heads_bias_grad = jnp.stack([jnp.sum(grad_query.astype(jnp.float32), axis=0), jnp.sum(grad_value.astype(jnp.float32), axis=0)])
    grad_proj = jnp.stack([grad_query, grad_key, grad_value], axis=1).astype(jnp.bfloat16)
    heads_weight_grad = jnp.einsum(
        "rd,rcn->dcn", first_low[:some], grad_proj, preferred_element_type=jnp.float32
    )
    first_share = jnp.einsum(
        "rcn,dcn->rd", grad_proj, qkv_weight, preferred_element_type=jnp.float32
    )
    grad_first = lax.psum(first_share.astype(jnp.bfloat16), "tensor").astype(jnp.float32)
    grad_first = jnp.pad(grad_first, ((0, rows - some), (0, 0)))
    gain1_grad = jnp.sum(grad_first * normed1, axis=0)
    shift1_grad = jnp.sum(grad_first, axis=0)
    stream_grad = (
        (grad_after + normalize_back(grad_first, normed1, inverse1, norm1_gain))
        .astype(jnp.bfloat16)
        .reshape(slots, length, width)
    )
    (
        gain1_grad,
        shift1_grad,
        heads_weight_grad,
        heads_bias_grad,
        merge_weight_grad,
        merge_bias_grad,
        scale1_grad,
        gain2_grad,
        shift2_grad,
        first_weight_grad,
        first_bias_grad,
        second_weight_grad,
        second_bias_grad,
        scale2_grad,
    ) = (
        lax.psum(gain1_grad.astype(jnp.bfloat16), "dp").astype(jnp.float32),
        lax.psum(shift1_grad.astype(jnp.bfloat16), "dp").astype(jnp.float32),
        lax.psum(heads_weight_grad.astype(jnp.bfloat16), "dp").astype(jnp.float32),
        lax.psum(heads_bias_grad.astype(jnp.bfloat16), "dp").astype(jnp.float32),
        lax.psum(merge_weight_grad.astype(jnp.bfloat16), "dp").astype(jnp.float32),
        lax.psum(merge_bias_grad.astype(jnp.bfloat16), "dp").astype(jnp.float32),
        lax.psum(scale1_grad.astype(jnp.bfloat16), "dp").astype(jnp.float32),
        lax.psum(gain2_grad.astype(jnp.bfloat16), "dp").astype(jnp.float32),
        lax.psum(shift2_grad.astype(jnp.bfloat16), "dp").astype(jnp.float32),
        lax.psum(first_weight_grad.astype(jnp.bfloat16), "dp").astype(jnp.float32),
        lax.psum(first_bias_grad.astype(jnp.bfloat16), "dp").astype(jnp.float32),
        lax.psum(second_weight_grad.astype(jnp.bfloat16), "dp").astype(jnp.float32),
        lax.psum(second_bias_grad.astype(jnp.bfloat16), "dp").astype(jnp.float32),
        lax.psum(scale2_grad.astype(jnp.bfloat16), "dp").astype(jnp.float32),
    )
    root_means = jnp.sqrt(square_sums / (slot_count * SEQ * width))
    return (
        block_output,
        stream_grad,
        gain1_grad,
        shift1_grad,
        heads_weight_grad,
        heads_bias_grad,
        merge_weight_grad,
        merge_bias_grad,
        scale1_grad,
        gain2_grad,
        shift2_grad,
        first_weight_grad,
        first_bias_grad,
        second_weight_grad,
        second_bias_grad,
        scale2_grad,
        root_means,
    )


def solution(mesh):
    return jax.shard_map(
        shards,
        mesh=mesh,
        in_specs=(
            P("dp", None, None),
            P("dp"),
            P(),
            P(),
            P(None, None, "tensor"),
            P(None, "tensor"),
            P("tensor", None),
            P(),
            P(),
            P(),
            P(),
            P(None, "tensor"),
            P("tensor"),
            P("tensor", None),
            P(),
            P(),
            P("dp", None, None),
        ),
        out_specs=(
            P("dp", None, None),
            P("dp", None, None),
            P(),
            P(),
            P(None, None, "tensor"),
            P(None, "tensor"),
            P("tensor", None),
            P(),
            P(),
            P(),
            P(),
            P(None, "tensor"),
            P("tensor"),
            P("tensor", None),
            P(),
            P(),
            P(),
        ),
        check_vma=False,
    )
```
